32 devices in a mesh: freq: 2 (over y), bfly: 16 (over z, x, core).
Axes of the slice: x: 2, y: 2, z: 4, core: 2. Of those that a mesh axis runs over, the one named last changes fastest.
Arguments:
- coefficients: bfloat16 [32768, 512], P(('freq', 'bfly')), parts along dimension 0, may hold values from -6 to 6
- transfer: bfloat16 [5, 32768, 1024], P(None, ('freq', 'bfly')), parts along dimension 1, may hold values from -0.25 to 0.25
- ranks: int32 [6, 16], P(None, 'bfly'), may hold values from 256 to 1024, as said below
- owner_map: int32 [16], replicated, may hold values from 0 to 3, as said below
Outputs:
- target_field: bfloat16 [8192, 512], P(('freq', 'bfly')), parts along dimension 0
The draws below stay inside these ranges and needn't reach their ends.
There are 2 independent parts, one for each index of `freq`. The reference program is written for one: setup_inputs(seed, part) draws one part's arguments, and reference() takes and returns one part's arrays. A program takes and returns all parts, laid end to end along the dimension named above; an argument that names none is the same for every part. Nothing has to cross between parts.
Inputs may be any that keep to these rules, and one draw needn't show every extreme that they name: Every row of ranks holds the value 1024 at least once. `owner_map`: within each aligned group of four blocks the four entries are a permutation of 0 to 3.
All inputs are finite; a program needn't handle non-finite values.
Results may differ from the reference program's by a relative error of at most 0.0095.
Values may be sent and summed in bfloat16 or wider, within the bound.
A program may use at most 64 MiB of HBM per device.

```python
import jax
import jax.numpy as jnp
import numpy as np
from jax import lax

R = 1024
W = 512
LEVELS = 5
NB = 16


def draw_ranks(key, part):
    base_key = jax.random.fold_in(key, 11)
    first_key, second_key, third_key = jax.random.split(base_key, 3)
    values = jax.random.randint(first_key, (LEVELS + 1, NB), R // 4, R + 1)
    top_pos = jax.random.randint(second_key, (LEVELS + 1, 1), 0, NB)
    low_pos = jax.random.randint(third_key, (LEVELS + 1, 1), 0, NB)
    columns = jnp.arange(NB)[None, :]
    values = jnp.where(columns == low_pos, R // 4, values)
    values = jnp.where(columns == top_pos, R, values)
    return values.astype(jnp.int32)


def draw_owner_map(key, part):
    base_key = jax.random.fold_in(key, 23)
    group_keys = jax.random.split(base_key, NB // 4)
    orders = jax.vmap(lambda one_key: jax.random.permutation(one_key, 4))(group_keys)
    last_row = (orders[-1] - orders[-1, 3] + 4) % 4
    orders = orders.at[-1].set(last_row)
    return orders.reshape(NB).astype(jnp.int32)


def shard_levels(key, extent, shards, smallest, high):
    level = 1.0
    for axis_at, blocks in shards:
        heights = jax.random.uniform(jax.random.fold_in(jax.random.fold_in(key, 6), axis_at), (blocks,), jnp.float32, smallest / len(shards), high / len(shards))
        level = level * jnp.repeat(jnp.exp(heights), extent[axis_at] // blocks).reshape((-1,) + (1,) * (len(extent) - 1 - axis_at))
    return level


def bell_draw(own_key, extent, spread, limit, shards=(), kind=jnp.bfloat16):
    loudness = shard_levels(own_key, extent, shards, -0.22, 0.18) if shards else 1.0
    drawn = jax.random.normal(own_key, extent, jnp.float32) * spread * loudness
    return jnp.minimum(jnp.maximum(drawn, -limit), limit).astype(kind)


def setup_inputs(seed: int = 0, part: int = 0) -> dict:
    key_list = jax.random.split(jax.random.key(seed), 5)
    own_keys = jax.random.split(jax.random.fold_in(key_list[4], part), 5)
    coefficients = bell_draw(own_keys[0], (NB * R, W), 1.0, 6.0, ((0, 16),))
    transfer = bell_draw(own_keys[1], (LEVELS, NB * R, R), (R // 2) ** -0.5, 0.25, ((1, 16),))
    ranks = draw_ranks(jax.random.fold_in(key_list[4], 71), part)
    owner_map = draw_owner_map(jax.random.fold_in(key_list[4], 71), part)
    return {"coefficients": coefficients, "transfer": transfer, "ranks": ranks, "owner_map": owner_map}


def block_product(operands):
    return jnp.dot(operands[0], operands[1], preferred_element_type=jnp.float32)


def reference(coefficients, transfer, ranks, owner_map):
    half_rows = R // 2
    log_count = NB.bit_length() - 1
    row_ids = jnp.arange(R, dtype=jnp.int32)
    blocks = np.arange(NB)
    current = coefficients.reshape(NB, R, W)
    live = row_ids[None, :] < ranks[0][:, None]
    current = jnp.where(live[:, :, None], current, jnp.zeros((), jnp.bfloat16))
    for level_idx in range(LEVELS):
        bit_pos = (log_count - 1 - level_idx) % log_count
        which_half = (blocks >> bit_pos) & 1
        low_blocks = blocks & ~(1 << bit_pos)
        high_blocks = blocks | (1 << bit_pos)
        halves = current.reshape(NB, half_rows, 2, W).transpose(0, 2, 1, 3)
        lower_half = halves[low_blocks, which_half]
        upper_half = halves[high_blocks, which_half]
        stacked = jnp.concatenate([lower_half, upper_half], axis=1)
        matrices = transfer[level_idx].reshape(NB, R, R)
        product = lax.map(block_product, (matrices, stacked))
        keep_rows = row_ids[None, :] < ranks[level_idx + 1][:, None]
        current = jnp.where(keep_rows[:, :, None], product, jnp.float32(0.0)).astype(jnp.bfloat16)
    totals = current.astype(jnp.float32).reshape(NB // 4, 4, R, W).sum(axis=1)
    quarters = totals.reshape(NB // 4, 4, R // 4, W)
    owners = owner_map.reshape(NB // 4, 4)
    group_ids = jnp.arange(NB // 4, dtype=jnp.int32)
    picked = quarters[group_ids[:, None], owners]
    return picked.reshape(NB * R // 4, W).astype(jnp.bfloat16)
```

```python
import functools

import jax
import jax.numpy as jnp
from jax import lax
from jax.experimental import pallas as pl
from jax.experimental.pallas import tpu as pltpu
from jax.sharding import PartitionSpec as P

LANES = 128
GROUP = 4
F32 = jnp.float32
BF16 = jnp.bfloat16


def schedule(levels, chunks):
    order = []
    arrive = [7.2, 12.5, 16.5, 18.5, 29.0]
    for c in range(chunks):
        for level in range(levels):
            base = arrive[level] if level < len(arrive) else arrive[-1] + level
            order.append((base + 5.6 * c, "level", level, c))
        order.append((arrive[-1] + 4.4 + 5.6 * c, "final", levels, c))
        order.append((0.0 if c < 2 else 7.3 + 5.6 * (c - 2), "first", -1, c))
    return sorted(order)


def kernel(levels, count, ranks, owners, coef, transfer, out, m, xin, ybuf, acc, zown, zsend, zrecv, yfin, fsend, frecv,
           m_sem, x_sem, z_ssem, z_rsem, f_ssem, f_rsem):
    rows, width = coef.shape
    half, quarter, chunks = rows // 2, rows // GROUP, width // LANES
    log_count = count.bit_length() - 1
    pos = lax.axis_index("bfly")
    bits = [(log_count - 1 - level) % log_count for level in range(levels)]

    def bit_of(b):
        return (pos // 2**b) % 2

    def partner(mask):
        where = pos
        for b in range(log_count):
            if mask >> b & 1:
                where = where + (1 - 2 * bit_of(b)) * 2**b
        return where

    x_copies = [pltpu.make_async_copy(coef.at[:, pl.ds(c * LANES, LANES)], xin.at[c], x_sem.at[c]) for c in range(chunks)]
    for copy in x_copies:
        copy.start()
    m_copies = []
    for level in range(levels):
        s = bit_of(bits[level])
        for side, start in ((0, s), (1, 1 - s)):
            cols = pl.ds(pl.multiple_of(start * half, half), half)
            copy = pltpu.make_async_copy(transfer.at[level, :, cols], m.at[level, side], m_sem.at[level, side])
            copy.start()
            m_copies.append(copy)
    masks = sorted({2**b for b in bits} | set(range(1, GROUP)))
    barrier = pltpu.get_barrier_semaphore()
    for mask in masks:
        pl.semaphore_signal(barrier, inc=1, device_id={"bfly": partner(mask)}, device_id_type=pl.DeviceIdType.MESH)
    pl.semaphore_wait(barrier, len(masks))

    loaded = set()

    def matrix(level, side):
        if (level, side) not in loaded:
            loaded.add((level, side))
            m_copies[2 * level + side].wait()
        return m[level, side]

    row_ids = lax.broadcasted_iota(jnp.int32, (rows, LANES), 0)
    z_copies, f_copies = {}, {}

    def spread(level, c, value):
        s = bit_of(bits[level])
        ybuf[...] = jnp.where(row_ids < ranks[level, 0], value, F32(0.0))
        even = ybuf[pl.ds(0, half, stride=2), :].astype(BF16)
        odd = ybuf[pl.ds(1, half, stride=2), :].astype(BF16)
        low = jnp.broadcast_to(s, even.shape) == 0
        zsend[level, c] = jnp.where(low, odd, even)
        copy = pltpu.make_async_remote_copy(
            zsend.at[level, c], zrecv.at[level, c], z_ssem.at[level, c], z_rsem.at[level, c],
            device_id={"bfly": partner(2 ** bits[level])}, device_id_type=pl.DeviceIdType.MESH)
        copy.start()
        z_copies[level, c] = copy
        zown[c] = jnp.where(low, even, odd)
        acc[c] = jnp.dot(matrix(level, 0), zown[c], preferred_element_type=F32)

    def owned(mask):
        return owners[(pos // GROUP) * GROUP + partner(mask) % GROUP]

    def picked(c, mask):
        which = jnp.full((quarter, LANES), owned(mask), jnp.int32)
        value = yfin[c, :quarter, :]
        for q in range(1, GROUP):
            value = jnp.where(which == q, yfin[c, q * quarter:(q + 1) * quarter, :], value)
        return value

    for _, kind, level, c in schedule(levels, chunks):
        if kind == "first":
            x_copies[c].wait()
            spread(0, c, xin[c].astype(F32))
        elif kind == "level":
            z_copies[level, c].wait_recv()
            product = acc[c] + jnp.dot(matrix(level, 1), zrecv[level, c], preferred_element_type=F32)
            if level + 1 < levels:
                spread(level + 1, c, product)
            else:
                kept = jnp.where(row_ids < ranks[levels, 0], product, F32(0.0))
                yfin[c] = kept.astype(BF16).astype(F32)
                for mask in range(GROUP - 1, 0, -1):
                    fsend[c, mask - 1] = picked(c, mask).astype(BF16)
                    copy = pltpu.make_async_remote_copy(
                        fsend.at[c, mask - 1], frecv.at[c, mask - 1], f_ssem.at[c, mask - 1], f_rsem.at[c, mask - 1],
                        device_id={"bfly": partner(mask)}, device_id_type=pl.DeviceIdType.MESH)
                    copy.start()
                    f_copies[c, mask] = copy
        else:
            total = picked(c, 0)
            for mask in range(1, GROUP):
                f_copies[c, mask].wait_recv()
                total = total + frecv[c, mask - 1].astype(F32)
            out[:, c * LANES:(c + 1) * LANES] = total.astype(BF16)
    for copy in list(z_copies.values()) + list(f_copies.values()):
        copy.wait_send()


def shards(coefficients, transfer, ranks, owner_map):
    rows, width = coefficients.shape
    levels = transfer.shape[0]
    count = lax.axis_size("bfly")
    half, quarter, chunks = rows // 2, rows // GROUP, width // LANES
    dma = pltpu.SemaphoreType.DMA
    return pl.pallas_call(
        functools.partial(kernel, levels, count),
        out_shape=jax.ShapeDtypeStruct((quarter, width), BF16),
        in_specs=[pl.BlockSpec(memory_space=pltpu.SMEM)] * 2 + [pl.BlockSpec(memory_space=pl.ANY)] * 2,
        out_specs=pl.BlockSpec(memory_space=pltpu.VMEM),
        scratch_shapes=[
            pltpu.VMEM((levels, 2, rows, half), BF16),
            pltpu.VMEM((chunks, rows, LANES), BF16),
            pltpu.VMEM((rows, LANES), F32),
            pltpu.VMEM((chunks, rows, LANES), F32),
            pltpu.VMEM((chunks, half, LANES), BF16),
            pltpu.VMEM((levels, chunks, half, LANES), BF16),
            pltpu.VMEM((levels, chunks, half, LANES), BF16),
            pltpu.VMEM((chunks, rows, LANES), F32),
            pltpu.VMEM((chunks, GROUP - 1, quarter, LANES), BF16),
            pltpu.VMEM((chunks, GROUP - 1, quarter, LANES), BF16),
            dma((levels, 2)),
            dma((chunks,)),
            dma((levels, chunks)),
            dma((levels, chunks)),
            dma((chunks, GROUP - 1)),
            dma((chunks, GROUP - 1)),
        ],
        compiler_params=pltpu.CompilerParams(collective_id=0, has_side_effects=True, vmem_limit_bytes=56 * 2**20),
    )(ranks, owner_map, coefficients, transfer)


def solution(mesh):
    in_specs = (P(("freq", "bfly"), None), P(None, ("freq", "bfly"), None), P(None, "bfly"), P())
    out_specs = P(("freq", "bfly"), None)
    return jax.shard_map(shards, mesh=mesh, in_specs=in_specs, out_specs=out_specs, check_vma=False)
```

```python
import functools

import jax
import jax.numpy as jnp
from jax import lax
from jax.experimental import pallas as pl
from jax.experimental.pallas import tpu as pltpu
from jax.sharding import PartitionSpec as P

LANES = 128
GROUP = 4
PIECES = 1
F32 = jnp.float32
BF16 = jnp.bfloat16


def schedule(levels, chunks):
    order = []
    arrive = [7.2, 12.9, 18.5, 21.5, 29.0]
    firsts = [0, 0, 7.3, 12.95]
    for c in range(chunks):
        for level in range(levels):
            at = arrive[level] if level < len(arrive) else arrive[-1] + level
            order.append((at + 5.6 * c, "level", level, c))
        order.append((arrive[-1] + 4.4 + 5.6 * c, "final", levels, c))
        order.append((firsts[c], "first", -1, c))
    return sorted(order)


def kernel(levels, count, ranks, owners, coef, transfer, out, m, xin, ybuf, acc, zown, zsend, zrecv, yfin, fsend, frecv,
           m_sem, x_sem, z_ssem, z_rsem, f_ssem, f_rsem):
    rows, width = coef.shape
    half, quarter, chunks = rows // 2, rows // GROUP, width // LANES
    log_count = count.bit_length() - 1
    pos = lax.axis_index("bfly")
    bits = [(log_count - 1 - level) % log_count for level in range(levels)]

    def bit_of(b):
        return (pos // 2**b) % 2

    def partner(mask):
        where = pos
        for b in range(log_count):
            if mask >> b & 1:
                where = where + (1 - 2 * bit_of(b)) * 2**b
        return where

    x_copies = [pltpu.make_async_copy(coef.at[:, pl.ds(c * LANES, LANES)], xin.at[c], x_sem.at[c]) for c in range(chunks)]
    for copy in x_copies:
        copy.start()
    m_copies = []
    for level in range(levels):
        s = bit_of(bits[level])
        for side, start in ((0, s), (1, 1 - s)):
            cols = pl.ds(pl.multiple_of(start * half, half), half)
            copy = pltpu.make_async_copy(transfer.at[level, :, cols], m.at[level, side], m_sem.at[level, side])
            copy.start()
            m_copies.append(copy)
    masks = sorted({2**b for b in bits} | set(range(1, GROUP)))
    barrier = pltpu.get_barrier_semaphore()
    for mask in masks:
        pl.semaphore_signal(barrier, inc=1, device_id={"bfly": partner(mask)}, device_id_type=pl.DeviceIdType.MESH)

    loaded = set()

    def matrix(level, side):
        if (level, side) not in loaded:
            loaded.add((level, side))
            m_copies[2 * level + side].wait()
        return m[level, side]

    part = rows // PIECES
    row_ids = lax.broadcasted_iota(jnp.int32, (part, LANES), 0)
    z_copies, f_copies = {}, {}

    def masked(level, piece, value):
        return jnp.where(row_ids < ranks[level] - piece * part, value, F32(0.0))

    def spread(level, c, rows_of_x):
        s = bit_of(bits[level])
        depth = part // 2
        for p in range(PIECES):
            at = pl.ds(p * depth, depth)
            ybuf[p] = masked(level, p, rows_of_x(pl.ds(p * part, part)))
            even = ybuf[p, pl.ds(0, depth, stride=2), :].astype(BF16)
            odd = ybuf[p, pl.ds(1, depth, stride=2), :].astype(BF16)
            low = jnp.broadcast_to(s, even.shape) == 0
            zsend[level, c, at] = jnp.where(low, odd, even)
            if not z_copies:
                pl.semaphore_wait(barrier, len(masks))
            copy = pltpu.make_async_remote_copy(
                zsend.at[level, c, at], zrecv.at[level, c, at], z_ssem.at[level, c, p], z_rsem.at[level, c, p],
                device_id={"bfly": partner(2 ** bits[level])}, device_id_type=pl.DeviceIdType.MESH)
            copy.start()
            z_copies[level, c, p] = copy
            zown[c, at] = jnp.where(low, even, odd)
        acc[c] = jnp.dot(matrix(level, 0), zown[c], preferred_element_type=F32)

    def owned(mask):
        return owners[(pos // GROUP) * GROUP + partner(mask) % GROUP]

    def picked(c, mask):
        which = jnp.full((quarter, LANES), owned(mask), jnp.int32)
        value = yfin[c, :quarter, :]
        for q in range(1, GROUP):
            value = jnp.where(which == q, yfin[c, q * quarter:(q + 1) * quarter, :], value)
        return value

    for _, kind, level, c in schedule(levels, chunks):
        if kind == "first":
            x_copies[c].wait()
            spread(0, c, lambda at: xin[c, at].astype(F32))
        elif kind == "level":
            for p in range(PIECES):
                z_copies[level, c, p].wait_recv()
            matrix(level, 1)

            def product(at):
                return acc[c, at] + jnp.dot(m[level, 1, at], zrecv[level, c], preferred_element_type=F32)

            if level + 1 < levels:
                spread(level + 1, c, product)
            else:
                for p in range(PIECES):
                    at = pl.ds(p * part, part)
                    yfin[c, at] = masked(levels, p, product(at)).astype(BF16).astype(F32)
                for mask in range(GROUP - 1, 0, -1):
                    fsend[c, mask - 1] = picked(c, mask).astype(BF16)
                    copy = pltpu.make_async_remote_copy(
                        fsend.at[c, mask - 1], frecv.at[c, mask - 1], f_ssem.at[c, mask - 1], f_rsem.at[c, mask - 1],
                        device_id={"bfly": partner(mask)}, device_id_type=pl.DeviceIdType.MESH)
                    copy.start()
                    f_copies[c, mask] = copy
        else:
            total = picked(c, 0)
            for mask in range(1, GROUP):
                f_copies[c, mask].wait_recv()
                total = total + frecv[c, mask - 1].astype(F32)
            out[:, c * LANES:(c + 1) * LANES] = total.astype(BF16)
    for copy in list(z_copies.values()) + list(f_copies.values()):
        copy.wait_send()


def shards(coefficients, transfer, ranks, owner_map):
    rows, width = coefficients.shape
    levels = transfer.shape[0]
    count = lax.axis_size("bfly")
    half, quarter, chunks = rows // 2, rows // GROUP, width // LANES
    dma = pltpu.SemaphoreType.DMA
    return pl.pallas_call(
        functools.partial(kernel, levels, count),
        out_shape=jax.ShapeDtypeStruct((quarter, width), BF16),
        in_specs=[pl.BlockSpec(memory_space=pltpu.SMEM)] * 2 + [pl.BlockSpec(memory_space=pl.ANY)] * 2,
        out_specs=pl.BlockSpec(memory_space=pltpu.VMEM),
        scratch_shapes=[
            pltpu.VMEM((levels, 2, rows, half), BF16),
            pltpu.VMEM((chunks, rows, LANES), BF16),
            pltpu.VMEM((PIECES, rows // PIECES, LANES), F32),
            pltpu.VMEM((chunks, rows, LANES), F32),
            pltpu.VMEM((chunks, half, LANES), BF16),
            pltpu.VMEM((levels, chunks, half, LANES), BF16),
            pltpu.VMEM((levels, chunks, half, LANES), BF16),
            pltpu.VMEM((chunks, rows, LANES), F32),
            pltpu.VMEM((chunks, GROUP - 1, quarter, LANES), BF16),
            pltpu.VMEM((chunks, GROUP - 1, quarter, LANES), BF16),
            dma((levels, 2)),
            dma((chunks,)),
            dma((levels, chunks, PIECES)),
            dma((levels, chunks, PIECES)),
            dma((chunks, GROUP - 1)),
            dma((chunks, GROUP - 1)),
        ],
        compiler_params=pltpu.CompilerParams(collective_id=0, has_side_effects=True, vmem_limit_bytes=56 * 2**20),
    )(ranks.reshape(-1), owner_map, coefficients, transfer)


def solution(mesh):
    in_specs = (P(("freq", "bfly"), None), P(None, ("freq", "bfly"), None), P(None, "bfly"), P())
    out_specs = P(("freq", "bfly"), None)
    return jax.shard_map(shards, mesh=mesh, in_specs=in_specs, out_specs=out_specs, check_vma=False)
```

```python
import functools

import jax
import jax.numpy as jnp
from jax import lax
from jax.experimental import pallas as pl
from jax.experimental.pallas import tpu as pltpu
from jax.sharding import PartitionSpec as P

LANES = 128
GROUP = 4
PIECES = 1
F32 = jnp.float32
BF16 = jnp.bfloat16


def schedule(levels, chunks):
    order = []
    arrive = [7.2, 12.9, 18.5, 21.5, 33.5]
    firsts = [0, 0, 7.3, 12.95]
    for c in range(chunks):
        for level in range(levels):
            at = arrive[level] if level < len(arrive) else arrive[-1] + level
            order.append((at + 5.6 * c, "level", level, c))
        order.append((arrive[-1] + 10.0 + 5.6 * c, "final", levels, c))
        order.append((firsts[c], "first", -1, c))
    return sorted(order)


def kernel(levels, count, ranks, owners, coef, transfer, out, m, xin, ybuf, acc, zown, zsend, zrecv, yfin, fsend, frecv,
           m_sem, x_sem, z_ssem, z_rsem, f_ssem, f_rsem):
    rows, width = coef.shape
    half, quarter, chunks = rows // 2, rows // GROUP, width // LANES
    log_count = count.bit_length() - 1
    pos = lax.axis_index("bfly")
    bits = [(log_count - 1 - level) % log_count for level in range(levels)]

    def bit_of(b):
        return (pos // 2**b) % 2

    def partner(mask):
        where = pos
        for b in range(log_count):
            if mask >> b & 1:
                where = where + (1 - 2 * bit_of(b)) * 2**b
        return where

    masks = sorted({2**b for b in bits} | set(range(1, GROUP)))
    barrier = pltpu.get_barrier_semaphore()
    for mask in masks:
        pl.semaphore_signal(barrier, inc=1, device_id={"bfly": partner(mask)}, device_id_type=pl.DeviceIdType.MESH)
    x_copies = [pltpu.make_async_copy(coef.at[:, pl.ds(c * LANES, LANES)], xin.at[c], x_sem.at[c]) for c in range(chunks)]
    for copy in x_copies:
        copy.start()
    m_copies = []
    for level in range(levels):
        s = bit_of(bits[level])
        for side, start in ((0, s), (1, 1 - s)):
            cols = pl.ds(pl.multiple_of(start * half, half), half)
            copy = pltpu.make_async_copy(transfer.at[level, :, cols], m.at[level, side], m_sem.at[level, side])
            m_copies.append(copy)
    loaded = set()

    def matrix(level, side):
        if (level, side) not in loaded:
            loaded.add((level, side))
            m_copies[2 * level + side].wait()
        return m[level, side]

    part = rows // PIECES
    row_ids = lax.broadcasted_iota(jnp.int32, (part, LANES), 0)
    z_copies, f_copies = {}, {}

    def masked(level, piece, value):
        return jnp.where(row_ids < ranks[level] - piece * part, value, F32(0.0))

    def spread(level, c, rows_of_x):
        s = bit_of(bits[level])
        depth = part // 2
        for p in range(PIECES):
            at = pl.ds(p * depth, depth)
            ybuf[p] = masked(level, p, rows_of_x(pl.ds(p * part, part)))
            even = ybuf[p, pl.ds(0, depth, stride=2), :].astype(BF16)
            odd = ybuf[p, pl.ds(1, depth, stride=2), :].astype(BF16)
            low = jnp.broadcast_to(s, even.shape) == 0
            zsend[level, c, at] = jnp.where(low, odd, even)
            if not z_copies:
                pl.semaphore_wait(barrier, len(masks))
            copy = pltpu.make_async_remote_copy(
                zsend.at[level, c, at], zrecv.at[level, c, at], z_ssem.at[level, c, p], z_rsem.at[level, c, p],
                device_id={"bfly": partner(2 ** bits[level])}, device_id_type=pl.DeviceIdType.MESH)
            copy.start()
            z_copies[level, c, p] = copy
            if len(z_copies) == 1:
                for load in m_copies:
                    load.start()
            zown[c, at] = jnp.where(low, even, odd)
        acc[c] = jnp.dot(matrix(level, 0), zown[c], preferred_element_type=F32)

    def owned(mask):
        return owners[(pos // GROUP) * GROUP + partner(mask) % GROUP]

    def picked(c, mask):
        which = jnp.full((quarter, LANES), owned(mask), jnp.int32)
        value = yfin[c, :quarter, :]
        for q in range(1, GROUP):
            value = jnp.where(which == q, yfin[c, q * quarter:(q + 1) * quarter, :], value)
        return value

    for _, kind, level, c in schedule(levels, chunks):
        if kind == "first":
            x_copies[c].wait()
            spread(0, c, lambda at: xin[c, at].astype(F32))
        elif kind == "level":
            for p in range(PIECES):
                z_copies[level, c, p].wait_recv()
            matrix(level, 1)

            def product(at):
                return acc[c, at] + jnp.dot(m[level, 1, at], zrecv[level, c], preferred_element_type=F32)

            if level + 1 < levels:
                spread(level + 1, c, product)
            else:
                for p in range(PIECES):
                    at = pl.ds(p * part, part)
                    yfin[c, at] = masked(levels, p, product(at)).astype(BF16).astype(F32)
                for mask in range(GROUP - 1, 0, -1):
                    fsend[c, mask - 1] = picked(c, mask).astype(BF16)
                    copy = pltpu.make_async_remote_copy(
                        fsend.at[c, mask - 1], frecv.at[c, mask - 1], f_ssem.at[c, mask - 1], f_rsem.at[c, mask - 1],
                        device_id={"bfly": partner(mask)}, device_id_type=pl.DeviceIdType.MESH)
                    copy.start()
                    f_copies[c, mask] = copy
        else:
            total = picked(c, 0)
            for mask in range(1, GROUP):
                f_copies[c, mask].wait_recv()
                total = total + frecv[c, mask - 1].astype(F32)
            out[:, c * LANES:(c + 1) * LANES] = total.astype(BF16)
    for copy in list(z_copies.values()) + list(f_copies.values()):
        copy.wait_send()


def shards(coefficients, transfer, ranks, owner_map):
    rows, width = coefficients.shape
    levels = transfer.shape[0]
    count = lax.axis_size("bfly")
    half, quarter, chunks = rows // 2, rows // GROUP, width // LANES
    dma = pltpu.SemaphoreType.DMA
    return pl.pallas_call(
        functools.partial(kernel, levels, count),
        out_shape=jax.ShapeDtypeStruct((quarter, width), BF16),
        in_specs=[pl.BlockSpec(memory_space=pltpu.SMEM)] * 2 + [pl.BlockSpec(memory_space=pl.ANY)] * 2,
        out_specs=pl.BlockSpec(memory_space=pltpu.VMEM),
        scratch_shapes=[
            pltpu.VMEM((levels, 2, rows, half), BF16),
            pltpu.VMEM((chunks, rows, LANES), BF16),
            pltpu.VMEM((PIECES, rows // PIECES, LANES), F32),
            pltpu.VMEM((chunks, rows, LANES), F32),
            pltpu.VMEM((chunks, half, LANES), BF16),
            pltpu.VMEM((levels, chunks, half, LANES), BF16),
            pltpu.VMEM((levels, chunks, half, LANES), BF16),
            pltpu.VMEM((chunks, rows, LANES), F32),
            pltpu.VMEM((chunks, GROUP - 1, quarter, LANES), BF16),
            pltpu.VMEM((chunks, GROUP - 1, quarter, LANES), BF16),
            dma((levels, 2)),
            dma((chunks,)),
            dma((levels, chunks, PIECES)),
            dma((levels, chunks, PIECES)),
            dma((chunks, GROUP - 1)),
            dma((chunks, GROUP - 1)),
        ],
        compiler_params=pltpu.CompilerParams(collective_id=0, has_side_effects=True, vmem_limit_bytes=56 * 2**20),
    )(ranks.reshape(-1), owner_map, coefficients, transfer)


def solution(mesh):
    in_specs = (P(("freq", "bfly"), None), P(None, ("freq", "bfly"), None), P(None, "bfly"), P())
    out_specs = P(("freq", "bfly"), None)
    return jax.shard_map(shards, mesh=mesh, in_specs=in_specs, out_specs=out_specs, check_vma=False)
```

```python
import functools

import jax
import jax.numpy as jnp
from jax import lax
from jax.experimental import pallas as pl
from jax.experimental.pallas import tpu as pltpu
from jax.sharding import PartitionSpec as P

LANES = 128
GROUP = 4
PIECES = 2
F32 = jnp.float32
BF16 = jnp.bfloat16


def schedule(levels, chunks):
    order = []
    arrive = [7.2, 12.9, 18.5, 21.5, 33.5]
    firsts = [0, 0, 7.3, 12.95]
    for c in range(chunks):
        for level in range(levels):
            at = arrive[level] if level < len(arrive) else arrive[-1] + level
            order.append((at + 5.6 * c, "level", level, c))
        order.append((arrive[-1] + 10.0 + 5.6 * c, "final", levels, c))
        order.append((firsts[c], "first", -1, c))
    return sorted(order)


def kernel(levels, count, ranks, owners, coef, transfer, out, m, xin, ybuf, acc, zown, zsend, zrecv, yfin, fsend, frecv,
           m_sem, x_sem, z_ssem, z_rsem, f_ssem, f_rsem):
    rows, width = coef.shape
    half, quarter, chunks = rows // 2, rows // GROUP, width // LANES
    log_count = count.bit_length() - 1
    pos = lax.axis_index("bfly")
    bits = [(log_count - 1 - level) % log_count for level in range(levels)]

    def bit_of(b):
        return (pos // 2**b) % 2

    def partner(mask):
        where = pos
        for b in range(log_count):
            if mask >> b & 1:
                where = where + (1 - 2 * bit_of(b)) * 2**b
        return where

    masks = sorted({2**b for b in bits} | set(range(1, GROUP)))
    barrier = pltpu.get_barrier_semaphore()
    for mask in masks:
        pl.semaphore_signal(barrier, inc=1, device_id={"bfly": partner(mask)}, device_id_type=pl.DeviceIdType.MESH)
    x_copies = [pltpu.make_async_copy(coef.at[:, pl.ds(c * LANES, LANES)], xin.at[c], x_sem.at[c]) for c in range(chunks)]
    for copy in x_copies:
        copy.start()
    m_copies = []
    for level in range(levels):
        s = bit_of(bits[level])
        for side, start in ((0, s), (1, 1 - s)):
            cols = pl.ds(pl.multiple_of(start * half, half), half)
            copy = pltpu.make_async_copy(transfer.at[level, :, cols], m.at[level, side], m_sem.at[level, side])
            m_copies.append(copy)
    loaded = set()

    def matrix(level, side):
        if (level, side) not in loaded:
            loaded.add((level, side))
            m_copies[2 * level + side].wait()
        return m[level, side]

    part = rows // PIECES
    row_ids = lax.broadcasted_iota(jnp.int32, (part, LANES), 0)
    z_copies, f_copies = {}, {}

    def masked(level, piece, value):
        return jnp.where(row_ids < ranks[level] - piece * part, value, F32(0.0))

    def spread(level, c, rows_of_x):
        s = bit_of(bits[level])
        depth = part // 2
        for p in range(PIECES):
            at = pl.ds(p * depth, depth)
            ybuf[p] = masked(level, p, rows_of_x(pl.ds(p * part, part)))
            even = ybuf[p, pl.ds(0, depth, stride=2), :].astype(BF16)
            odd = ybuf[p, pl.ds(1, depth, stride=2), :].astype(BF16)
            low = jnp.broadcast_to(s, even.shape) == 0
            zsend[level, c, at] = jnp.where(low, odd, even)
            if not z_copies:
                pl.semaphore_wait(barrier, len(masks))
            copy = pltpu.make_async_remote_copy(
                zsend.at[level, c, at], zrecv.at[level, c, at], z_ssem.at[level, c, p], z_rsem.at[level, c, p],
                device_id={"bfly": partner(2 ** bits[level])}, device_id_type=pl.DeviceIdType.MESH)
            copy.start()
            z_copies[level, c, p] = copy
            if len(z_copies) == 1:
                for load in m_copies:
                    load.start()
            zown[c, at] = jnp.where(low, even, odd)
        acc[c] = jnp.dot(matrix(level, 0), zown[c], preferred_element_type=F32)

    def owned(mask):
        return owners[(pos // GROUP) * GROUP + partner(mask) % GROUP]

    def picked(c, mask):
        which = jnp.full((quarter, LANES), owned(mask), jnp.int32)
        value = yfin[c, :quarter, :]
        for q in range(1, GROUP):
            value = jnp.where(which == q, yfin[c, q * quarter:(q + 1) * quarter, :], value)
        return value

    for _, kind, level, c in schedule(levels, chunks):
        if kind == "first":
            x_copies[c].wait()
            spread(0, c, lambda at: xin[c, at].astype(F32))
        elif kind == "level":
            for p in range(PIECES):
                z_copies[level, c, p].wait_recv()
            matrix(level, 1)

            def product(at):
                return acc[c, at] + jnp.dot(m[level, 1, at], zrecv[level, c], preferred_element_type=F32)

            if level + 1 < levels:
                spread(level + 1, c, product)
            else:
                for p in range(PIECES):
                    at = pl.ds(p * part, part)
                    yfin[c, at] = masked(levels, p, product(at)).astype(BF16).astype(F32)
                for mask in range(GROUP - 1, 0, -1):
                    fsend[c, mask - 1] = picked(c, mask).astype(BF16)
                    copy = pltpu.make_async_remote_copy(
                        fsend.at[c, mask - 1], frecv.at[c, mask - 1], f_ssem.at[c, mask - 1], f_rsem.at[c, mask - 1],
                        device_id={"bfly": partner(mask)}, device_id_type=pl.DeviceIdType.MESH)
                    copy.start()
                    f_copies[c, mask] = copy
        else:
            total = picked(c, 0)
            for mask in range(1, GROUP):
                f_copies[c, mask].wait_recv()
                total = total + frecv[c, mask - 1].astype(F32)
            out[:, c * LANES:(c + 1) * LANES] = total.astype(BF16)
    for copy in list(z_copies.values()) + list(f_copies.values()):
        copy.wait_send()


def shards(coefficients, transfer, ranks, owner_map):
    rows, width = coefficients.shape
    levels = transfer.shape[0]
    count = lax.axis_size("bfly")
    half, quarter, chunks = rows // 2, rows // GROUP, width // LANES
    dma = pltpu.SemaphoreType.DMA
    return pl.pallas_call(
        functools.partial(kernel, levels, count),
        out_shape=jax.ShapeDtypeStruct((quarter, width), BF16),
        in_specs=[pl.BlockSpec(memory_space=pltpu.SMEM)] * 2 + [pl.BlockSpec(memory_space=pl.ANY)] * 2,
        out_specs=pl.BlockSpec(memory_space=pltpu.VMEM),
        scratch_shapes=[
            pltpu.VMEM((levels, 2, rows, half), BF16),
            pltpu.VMEM((chunks, rows, LANES), BF16),
            pltpu.VMEM((PIECES, rows // PIECES, LANES), F32),
            pltpu.VMEM((chunks, rows, LANES), F32),
            pltpu.VMEM((chunks, half, LANES), BF16),
            pltpu.VMEM((levels, chunks, half, LANES), BF16),
            pltpu.VMEM((levels, chunks, half, LANES), BF16),
            pltpu.VMEM((chunks, rows, LANES), F32),
            pltpu.VMEM((chunks, GROUP - 1, quarter, LANES), BF16),
            pltpu.VMEM((chunks, GROUP - 1, quarter, LANES), BF16),
            dma((levels, 2)),
            dma((chunks,)),
            dma((levels, chunks, PIECES)),
            dma((levels, chunks, PIECES)),
            dma((chunks, GROUP - 1)),
            dma((chunks, GROUP - 1)),
        ],
        compiler_params=pltpu.CompilerParams(collective_id=0, has_side_effects=True, vmem_limit_bytes=56 * 2**20),
    )(ranks.reshape(-1), owner_map, coefficients, transfer)


def solution(mesh):
    in_specs = (P(("freq", "bfly"), None), P(None, ("freq", "bfly"), None), P(None, "bfly"), P())
    out_specs = P(("freq", "bfly"), None)
    return jax.shard_map(shards, mesh=mesh, in_specs=in_specs, out_specs=out_specs, check_vma=False)
```
